512 devices in a mesh: tok: 128 (over z, y, core), head: 4 (over x).
Axes of the slice: x: 4, y: 8, z: 8, core: 2. Of those that a mesh axis runs over, the one named last changes fastest.
Arguments:
- tokens: bfloat16 [16384, 1536], P('tok'), may hold values from -6 to 6
- norm_gain: bfloat16 [1536], replicated, may hold values from 0.099609375 to 1.8984375
- w_query: bfloat16 [1536, 1536], P('tok', 'head')
- w_keyval: bfloat16 [1536, 256], P('tok')
- w_out: bfloat16 [1536, 1536], P('head', 'tok'), may hold values from -0.5 to 0.5
- segment_ids: int32 [16384], P('tok'), may hold values from 0 to 30, as said below
- lengths: int32 [31], replicated, may hold values from 128 to 1024, as said below
- member_prompt: int32 [384], P('head'), may hold values from 0 to 30
Outputs:
- mixed: bfloat16 [16384, 1536], P('tok', 'head')
- cycle_cache: bfloat16 [384, 1024, 256], P('head', 'tok')
The draws below stay inside these ranges and needn't reach their ends.
Inputs may be any that keep to these rules, and one draw needn't show every extreme that they name: The prompts lie end to end in the order of lengths and their lengths sum to 16384; one prompt has exactly 1024 tokens and one exactly 128. `segment_ids`: segment_ids_t is the prompt that holds token t under lengths, so it never falls.
All inputs are finite; a program needn't handle non-finite values.
Results may differ from the reference program's by a relative error of at most 0.013.
Values may be sent and summed in bfloat16 or wider, within the bound.
No kernel may reach another device: no remote copies, remote signals or barrier semaphores. Data moves between devices by JAX's collectives and lax.ppermute only.
A program may use at most 64 MiB of HBM per device.

```python
import math
import jax
import jax.numpy as jnp
from jax import lax

D = 1536
NQ = 12
HD = 128
WINDOW = 1024
TOKENS = 16384
MAXLEN = 1024
MINLEN = 128
PROMPTS = 31
MEMBERS = 384


def prompt_lengths(key):
    others = PROMPTS - 2
    spare = TOKENS - MAXLEN - MINLEN - others * MINLEN
    weights = jax.random.randint(jax.random.fold_in(key, 7), (others,), 50, 101).astype(jnp.int32)
    shares = spare * weights // jnp.sum(weights)
    leftover = spare - jnp.sum(shares)
    shares = shares + (jnp.arange(others, dtype=jnp.int32) < leftover).astype(jnp.int32)
    listed = jnp.concatenate([jnp.array([MAXLEN, MINLEN], jnp.int32), MINLEN + shares.astype(jnp.int32)])
    order = jax.random.permutation(jax.random.fold_in(key, 9), PROMPTS)
    return listed[order].astype(jnp.int32)


def keyval_matrix(key):
    return jax.random.normal(jax.random.fold_in(key, 11), (D, 2 * HD), jnp.float32) / math.sqrt(D)


def draw_lengths(key, part):
    return prompt_lengths(jax.random.fold_in(key, 3))


def draw_segment_ids(key, part):
    counts = prompt_lengths(jax.random.fold_in(key, 3))
    prompt_ends = jnp.cumsum(counts).astype(jnp.int32)
    token_index = jnp.arange(TOKENS, dtype=jnp.int32)
    return jnp.sum((token_index[:, None] >= prompt_ends[None, :]).astype(jnp.int32), axis=1).astype(jnp.int32)


def draw_w_keyval(key, part):
    return keyval_matrix(key).astype(jnp.bfloat16)


def draw_w_query(key, part):
    drawn = jax.random.normal(jax.random.fold_in(key, 12), (D, NQ * HD), jnp.float32) / math.sqrt(D)
    return drawn.astype(jnp.bfloat16)


def place_ends(values, rng, low, top_value):
    index_at = [jax.random.randint(jax.random.fold_in(rng, axis), (), 0, length) for axis, length in enumerate(values.shape)]
    longest = values.shape.index(max(values.shape))
    next_to = index_at[:longest] + [(index_at[longest] + 1) % values.shape[longest]] + index_at[longest + 1:]
    return values.at[tuple(index_at)].set(low).at[tuple(next_to)].set(top_value)


def shard_levels(stream_key, dims, split, smallest, high):
    def one(position, parts):
        steps = jax.random.uniform(jax.random.fold_in(jax.random.fold_in(stream_key, 6), position), (parts,), jnp.float32, smallest / len(split), high / len(split))
        return jnp.repeat(jnp.exp(steps), dims[position] // parts).reshape((-1,) + (1,) * (len(dims) - position - 1))

    gain = one(*split[0])
    for cut in split[1:]:
        gain = gain * one(*cut)
    return gain


def noise(rng, extent, deviation, limit, pieces=(), kind=jnp.bfloat16):
    result = deviation * jax.random.normal(rng, extent, jnp.float32)
    if pieces:
        result = result * shard_levels(rng, extent, pieces, -0.22, 0.18)
    return jnp.clip(result, -limit, limit).astype(kind)


def setup_inputs(seed: int = 0) -> dict:
    key_list = jax.random.split(jax.random.key(seed), 9)
    tokens = noise(key_list[0], (TOKENS, D), 1.0, 6.0, ((0, 128),))
    norm_gain = jnp.clip(1.0 + 0.18 * jax.random.normal(key_list[1], (D,), jnp.float32), 0.099609375, 1.8984375).astype(jnp.bfloat16)
    w_query = draw_w_query(jax.random.fold_in(key_list[8], 71), 0)
    w_keyval = draw_w_keyval(jax.random.fold_in(key_list[8], 71), 0)
    w_out = noise(key_list[4], (NQ * HD, D), HD ** -0.5, 0.5, ((0, 4), (1, 128)))
    segment_ids = draw_segment_ids(jax.random.fold_in(key_list[8], 71), 0)
    lengths = draw_lengths(jax.random.fold_in(key_list[8], 71), 0)
    member_prompt = place_ends(jax.random.randint(key_list[7], (MEMBERS,), 0, PROMPTS), jax.random.fold_in(key_list[7], 1), 0, PROMPTS - 1).astype(jnp.int32)
    return dict(tokens=tokens, norm_gain=norm_gain, w_query=w_query, w_keyval=w_keyval, w_out=w_out, segment_ids=segment_ids, lengths=lengths, member_prompt=member_prompt)


def rotate(values, positions):
    half_width = values.shape[-1] // 2
    frequency = 10000.0 ** (-(jnp.arange(half_width, dtype=jnp.float32) * 2.0 / values.shape[-1]))
    angles = positions.astype(jnp.float32)[:, None] * frequency[None, :]
    cosine = jnp.cos(angles)[:, None, :]
    sine_values = jnp.sin(angles)[:, None, :]
    front_half = values[..., :half_width]
    back_half = values[..., half_width:]
    return jnp.concatenate([front_half * cosine - back_half * sine_values, back_half * cosine + front_half * sine_values], axis=-1)

def reference(tokens, norm_gain, w_query, w_keyval, w_out, segment_ids, lengths, member_prompt):
    widened = tokens.astype(jnp.float32)
    normed = (widened * lax.rsqrt(lax.optimization_barrier(jnp.mean(widened * widened, axis=1, keepdims=True)) + 1e-06) * norm_gain.astype(jnp.float32)).astype(jnp.bfloat16)
    prompt_ends = jnp.cumsum(lengths).astype(jnp.int32)
    starts = (prompt_ends - lengths).astype(jnp.int32)
    segments = segment_ids.astype(jnp.int32)
    positions = (jnp.arange(TOKENS, dtype=jnp.int32) - starts[segments]).astype(jnp.int32)
    queries = jnp.dot(normed, w_query, preferred_element_type=jnp.float32).reshape(TOKENS, NQ, HD)
    queries = rotate(queries, positions).astype(jnp.bfloat16)
    keyval = jnp.dot(normed, w_keyval, preferred_element_type=jnp.float32)
    rotated = rotate(keyval[:, None, :HD], positions)[:, 0]
    pairs = jnp.concatenate([rotated, keyval[:, HD:]], axis=1).astype(jnp.bfloat16)
    padded = jnp.concatenate([jnp.zeros((WINDOW, 2 * HD), jnp.bfloat16), pairs], axis=0)
    seg_padded = jnp.concatenate([jnp.full((WINDOW,), -1, jnp.int32), segments])
    query_block = min(512, TOKENS)
    score_scale = 1.0 / math.sqrt(HD)

    def attend(block_index):
        begin = (block_index * query_block).astype(jnp.int32)
        block_queries = lax.dynamic_slice_in_dim(queries, begin, query_block, 0).astype(jnp.float32)
        block_pairs = lax.dynamic_slice_in_dim(padded, begin, WINDOW + query_block, 0).astype(jnp.float32)
        query_seg = lax.dynamic_slice_in_dim(segments, begin, query_block, 0)
        key_seg = lax.dynamic_slice_in_dim(seg_padded, begin, WINDOW + query_block, 0)
        query_index = begin + jnp.arange(query_block, dtype=jnp.int32)
        key_index = begin - WINDOW + jnp.arange(WINDOW + query_block, dtype=jnp.int32)
        scores = jnp.einsum('qhd,kd->hqk', block_queries, block_pairs[:, :HD]) * score_scale
        allowed = (key_seg[None, :] == query_seg[:, None]) & (key_index[None, :] <= query_index[:, None])
        allowed = allowed & (key_index[None, :] > query_index[:, None] - WINDOW) & (key_index[None, :] >= 0)
        scores = jnp.where(allowed[None], scores, -jnp.inf)
        largest = lax.optimization_barrier(jnp.max(scores, axis=-1, keepdims=True))
        weights = jnp.exp(scores - largest)
        total = lax.optimization_barrier(jnp.sum(weights, axis=-1, keepdims=True))
        probs = lax.optimization_barrier(weights.astype(jnp.bfloat16)).astype(jnp.float32)
        mixed_values = jnp.einsum('hqk,kd->hqd', probs, block_pairs[:, HD:]) / total
        return jnp.transpose(mixed_values, (1, 0, 2)).reshape(query_block, NQ * HD).astype(jnp.bfloat16)
    attention = lax.map(attend, jnp.arange(TOKENS // query_block, dtype=jnp.int32)).reshape(TOKENS, NQ * HD)
    mixed = (widened + jnp.dot(attention, w_out, preferred_element_type=jnp.float32)).astype(jnp.bfloat16)
    members = member_prompt.astype(jnp.int32)
    base = (lengths[members] - WINDOW).astype(jnp.int32)
    slot_index = jnp.arange(WINDOW, dtype=jnp.int32)
    places = base[:, None] + jnp.mod(slot_index[None, :] - base[:, None], WINDOW)
    token_index = (starts[members][:, None] + places).astype(jnp.int32)
    fetched = pairs[jnp.clip(token_index, 0, TOKENS - 1)]
    cycle_cache = jnp.where((places >= 0)[..., None], fetched, jnp.zeros((), jnp.bfloat16))
    return (mixed, cycle_cache)
```

```python
import math

import jax
import jax.numpy as jnp
from jax import lax
from jax.sharding import Mesh, PartitionSpec as P

HD = 128
WINDOW = 1024
TOK = ("zh", "zl", "yh", "yl", "c")
PAD = 16
BF = jnp.bfloat16
F32 = jnp.float32


def ring(x, axes, step):
    size = lax.axis_size(axes)
    return lax.ppermute(x, axes, [(i, (i + step) % size) for i in range(size)])


def swap(x):
    return lax.ppermute(x, "c", [(0, 1), (1, 0)])


def earlier(x, distance):
    size = lax.axis_size(TOK)
    return lax.ppermute(x, TOK, [(i, i + distance) for i in range(size - distance)])


def gather_rows(chunk):
    near_y, near_z = ("yh", "yl"), ("zh", "zl")
    members = lax.axis_size(("zh", "yh"))
    half, quarter = members // 2, members // 4
    own = lax.all_to_all(
        jnp.broadcast_to(chunk[None], (members,) + chunk.shape), ("zh", "yh"), 0, 0, tiled=True
    )
    by_y = [ring(own[:half], near_y, 1), ring(own[half:], near_y, -1)]
    by_z = [ring(own[:half], near_z, 1), ring(own[half:], near_z, -1)]
    own_swapped = swap(own)
    diagonal = [
        ring(by_z[0][:quarter], near_y, 1),
        ring(by_z[0][quarter:], near_y, -1),
        ring(by_y[1][:quarter], near_z, 1),
        ring(by_y[1][quarter:], near_z, -1),
    ]
    sides = jnp.concatenate(by_y + by_z, axis=0)
    sides_swapped = swap(sides)
    corner = jnp.concatenate(diagonal, axis=0)
    corner_swapped = swap(corner)
    parts = [own, sides, corner, own_swapped, sides_swapped, corner_swapped]
    return jnp.concatenate(parts, axis=0).reshape(-1, chunk.shape[-1])


def gathered_index(devices, rows):
    zl, yl, core = lax.axis_index("zl"), lax.axis_index("yl"), lax.axis_index("c")
    n_yh = lax.axis_size("yh")
    per_class = lax.axis_size("zh") * n_yh
    place = jnp.arange(devices * PAD, dtype=jnp.int32)
    row = place % PAD
    member = (place // PAD) % per_class
    zh, yh = member // n_yh, member % n_yh
    group = (place // (PAD * per_class)) % 4
    other_z, other_y = group // 2, group % 2
    other_core = place // (PAD * per_class * 4)
    z = 2 * zh + (zl ^ other_z)
    y = 2 * yh + (yl ^ other_y)
    device = (z * (2 * n_yh) + y) * 2 + (core ^ other_core)
    return jnp.where(row < rows, device * rows + row, -1)


def per_device(tokens, norm_gain, w_query, w_keyval, w_out, segment_ids, lengths, member_prompt):
    shard_rows, width = tokens.shape
    q_cols = w_query.shape[1]
    kv_cols = w_keyval.shape[1]
    heads_here = q_cols // HD
    devices = lax.axis_size(TOK)
    n_head = lax.axis_size("head")
    tok_index = lax.axis_index(TOK)
    head_index = lax.axis_index("head")
    prompts = lengths.shape[0]
    w_rows = w_query.shape[0]

    chunk = jnp.concatenate([w_query, w_keyval, w_out.T], axis=1)
    chunk = jnp.pad(chunk, ((0, PAD - w_rows), (0, 0)))
    gathered = gather_rows(chunk)

    prompt_ends = jnp.cumsum(lengths)
    starts = prompt_ends - lengths
    global_index = tok_index * shard_rows + jnp.arange(shard_rows, dtype=jnp.int32)
    prompt_index = jnp.arange(prompts, dtype=jnp.int32)
    start_here = jnp.sum(
        jnp.where(segment_ids[:, None] == prompt_index[None, :], starts[None, :], 0), axis=1
    )
    positions = global_index - start_here
    frequency = 10000.0 ** (-(jnp.arange(HD // 2, dtype=F32) * 2.0 / HD))
    angles = positions.astype(F32)[:, None] * frequency[None, :]
    cosine, sine = jnp.cos(angles), jnp.sin(angles)
    cos_full = jnp.concatenate([cosine, cosine], axis=1)
    sin_full = jnp.concatenate([-sine, sine], axis=1)

    def rotate(values):
        swapped = jnp.concatenate([values[:, HD // 2 :], values[:, : HD // 2]], axis=1)
        return values * cos_full + swapped * sin_full

    widened = tokens.astype(F32)
    normed = (
        widened
        * lax.rsqrt(jnp.mean(widened * widened, axis=1, keepdims=True) + 1e-06)
        * norm_gain.astype(F32)
    ).astype(BF)
    order = gathered_index(devices, w_rows)
    placing = (jnp.arange(width, dtype=jnp.int32)[:, None] == order[None, :]).astype(BF)
    placed = jnp.dot(normed, placing, preferred_element_type=F32).astype(BF)
    projected = jnp.dot(placed, gathered[:, : q_cols + kv_cols], preferred_element_type=F32)
    keyval = projected[:, q_cols:]
    pairs = jnp.concatenate([rotate(keyval[:, :HD]), keyval[:, HD:]], axis=1).astype(BF)

    chip_reach = -(-WINDOW // (2 * shard_rows))
    behind = [earlier(pairs, 2 * k) for k in range(chip_reach, 0, -1)] + [pairs]
    own_keys = jnp.concatenate(behind, axis=0)
    other_keys = swap(own_keys)
    all_pairs = jnp.concatenate([own_keys, other_keys], axis=0)
    core = lax.axis_index("c")
    own_chip = tok_index // 2
    key_place = jnp.arange(2 * (chip_reach + 1) * shard_rows, dtype=jnp.int32)
    key_block = key_place // shard_rows
    key_chip = own_chip - chip_reach + key_block % (chip_reach + 1)
    key_core = core ^ (key_block // (chip_reach + 1))
    key_index = (2 * key_chip + key_core) * shard_rows + key_place % shard_rows

    queries = jnp.concatenate(
        [rotate(projected[:, s * HD : (s + 1) * HD]) for s in range(heads_here)], axis=0
    ).astype(BF)
    scores = lax.dot_general(
        queries, all_pairs[:, :HD], (((1,), (1,)), ((), ())), preferred_element_type=F32
    ) * (1.0 / math.sqrt(HD))
    allowed = (
        (key_index[None, :] >= start_here[:, None])
        & (key_index[None, :] <= global_index[:, None])
        & (key_index[None, :] > global_index[:, None] - WINDOW)
        & (key_index[None, :] >= 0)
    )
    scores = scores.reshape(heads_here, shard_rows, -1)
    scores = jnp.where(allowed[None], scores, -jnp.inf)
    largest = jnp.max(scores, axis=2, keepdims=True)
    weights = jnp.exp(scores - largest)
    total = jnp.sum(weights, axis=2, keepdims=True)
    probs = weights.astype(BF).reshape(heads_here * shard_rows, -1)
    summed = jnp.dot(probs, all_pairs[:, HD:], preferred_element_type=F32)
    attention = (summed / total.reshape(-1, 1)).astype(BF)
    attention = jnp.concatenate(
        [attention[s * shard_rows : (s + 1) * shard_rows] for s in range(heads_here)], axis=1
    )

    slots_here = WINDOW // devices
    col_share = kv_cols // n_head
    first_segment = jnp.sum((prompt_ends <= tok_index * shard_rows).astype(jnp.int32))
    slot_index = jnp.arange(WINDOW, dtype=jnp.int32)
    share = lax.dynamic_slice_in_dim(pairs, head_index * col_share, col_share, 1)
    pieces = []
    for local_seg in range(2):
        prompt_here = first_segment + local_seg
        matches = prompt_index == prompt_here
        prompt_size = jnp.sum(jnp.where(matches, lengths, 0))
        prompt_start = jnp.sum(jnp.where(matches, starts, 0))
        lowest = prompt_size - WINDOW
        places = lowest + jnp.mod(slot_index - lowest, WINDOW)
        local_rows = prompt_start + places - tok_index * shard_rows
        usable = (prompt_here < prompts) & (places >= 0)
        local_rows = jnp.where(usable, local_rows, -1)
        pick = (local_rows[:, None] == jnp.arange(shard_rows, dtype=jnp.int32)[None, :]).astype(BF)
        pieces.append(jnp.dot(pick, share, preferred_element_type=F32).astype(BF))
    outgoing = jnp.concatenate(pieces, axis=1).reshape(devices, slots_here, 2 * col_share)
    incoming = lax.all_to_all(outgoing, TOK, 0, 0, tiled=True)
    source_rows = jnp.arange(devices, dtype=jnp.int32) * shard_rows
    source_first = jnp.sum((prompt_ends[None, :] <= source_rows[:, None]).astype(jnp.int32), axis=1)
    table_rows = 32
    table_index = jnp.arange(table_rows, dtype=jnp.int32)
    table = jnp.zeros((table_rows, slots_here, col_share), F32)
    for local_seg in range(2):
        chooser = (source_first[None, :] + local_seg == table_index[:, None]).astype(BF)
        table = table + jnp.einsum(
            "ps,sjl->pjl",
            chooser,
            incoming[:, :, local_seg * col_share : (local_seg + 1) * col_share],
            preferred_element_type=F32,
        )
    table = table.astype(BF).reshape(shard_rows, -1)

    partial_out = lax.dot_general(
        attention, gathered[:, q_cols + kv_cols :], (((1,), (1,)), ((), ())), preferred_element_type=F32
    ).astype(BF)
    partial_out = lax.dot_general(
        partial_out, placing, (((1,), (1,)), ((), ())), preferred_element_type=F32
    ).astype(BF)
    quarter_cols = width // n_head
    sending = jnp.stack(
        [
            jnp.concatenate([partial_out[:, k * quarter_cols : (k + 1) * quarter_cols], table], axis=1)
            for k in range(n_head)
        ]
    )
    arrived = lax.all_to_all(sending, "head", 0, 0, tiled=True)
    residual = lax.dynamic_slice_in_dim(tokens, head_index * quarter_cols, quarter_cols, 1)
    mixed = (
        residual.astype(F32) + jnp.sum(arrived[:, :, :quarter_cols].astype(F32), axis=0)
    ).astype(BF)

    slot_table = arrived[:, :, quarter_cols:].reshape(n_head, table_rows, slots_here, col_share)
    member_pick = (member_prompt[:, None] == table_index[None, :]).astype(BF)
    cycle_cache = jnp.einsum("mp,hpjl->mjhl", member_pick, slot_table, preferred_element_type=F32)
    cycle_cache = cycle_cache.astype(BF).reshape(member_prompt.shape[0], slots_here, kv_cols)
    return (mixed, cycle_cache)


def solution(mesh):
    cut = Mesh(mesh.devices.reshape(4, 2, 4, 2, 2, 4), TOK + ("head",))
    return jax.shard_map(
        per_device,
        mesh=cut,
        in_specs=(
            P(TOK, None),
            P(),
            P(TOK, "head"),
            P(TOK, None),
            P("head", TOK),
            P(TOK),
            P(),
            P("head"),
        ),
        out_specs=(P(TOK, "head"), P("head", TOK, None)),
        check_vma=False,
    )
```

```python
import math

import jax
import jax.numpy as jnp
from jax import lax
from jax.sharding import Mesh, PartitionSpec as P


HD = 128
WINDOW = 1024
TOK = ("zh", "zl", "yh", "yl", "c")
BF = jnp.bfloat16
F32 = jnp.float32


def ring(x, axes, step):
    size = lax.axis_size(axes)
    return lax.ppermute(x, axes, [(i, (i + step) % size) for i in range(size)])


def swap(x):
    return lax.ppermute(x, "c", [(0, 1), (1, 0)])


def earlier(x, distance):
    size = lax.axis_size(TOK)
    return lax.ppermute(x, TOK, [(i, i + distance) for i in range(size - distance)])


def gather_rows(chunk):
    line = ("zh", "zl", "yh")
    members = lax.axis_size(line)
    n_zh = lax.axis_size("zh")
    half = members // 2
    own = lax.all_to_all(
        jnp.broadcast_to(chunk[None], (members,) + chunk.shape), line, 0, 0, tiled=True
    )
    below = ring(own[:half], ("yh", "yl"), 1)
    above = ring(own[half:], ("yh", "yl"), -1)
    own_swapped = swap(own)
    sides = jnp.concatenate([below, above], axis=0)
    sides_swapped = swap(sides)
    shape = (n_zh, members // n_zh) + chunk.shape
    pieces = [piece.reshape(shape) for piece in (own, sides, own_swapped, sides_swapped)]
    return jnp.stack(pieces, axis=1)


def block_places(rows, offset, stacked):
    yl, core = lax.axis_index("yl"), lax.axis_index("c")
    n_zl, n_yh = lax.axis_size("zl"), lax.axis_size("yh")
    place = jnp.arange(4 * n_zl * n_yh * stacked, dtype=jnp.int32)
    row = place % stacked - offset
    yh = (place // stacked) % n_yh
    zl = (place // (stacked * n_yh)) % n_zl
    piece = place // (stacked * n_yh * n_zl)
    y = 2 * yh + (yl ^ (piece % 2))
    device = (zl * (2 * n_yh) + y) * 2 + (core ^ (piece // 2))
    return jnp.where((row >= 0) & (row < rows), device * rows + row, -1)


def layer(tokens, norm_gain, w_query, w_keyval, w_out, segment_ids, lengths, member_prompt):
    shard_rows, width = tokens.shape
    q_cols = w_query.shape[1]
    kv_cols = w_keyval.shape[1]
    heads_here = q_cols // HD
    devices = lax.axis_size(TOK)
    n_head = lax.axis_size("head")
    tok_index = lax.axis_index(TOK)
    head_index = lax.axis_index("head")
    prompts = lengths.shape[0]
    w_rows = w_query.shape[0]

    upper = jnp.concatenate([w_query, w_keyval[:, :HD]], axis=1)
    lower = jnp.concatenate([w_keyval[:, HD:], w_out.T], axis=1)
    chunk = jnp.concatenate([upper, lower], axis=0)
    blocks = lax.axis_size("zh")
    gathered = gather_rows(chunk).reshape(-1, chunk.shape[1])

    prompt_ends = jnp.cumsum(lengths)
    starts = prompt_ends - lengths
    global_index = tok_index * shard_rows + jnp.arange(shard_rows, dtype=jnp.int32)
    prompt_index = jnp.arange(prompts, dtype=jnp.int32)
    start_here = jnp.sum(
        jnp.where(segment_ids[:, None] == prompt_index[None, :], starts[None, :], 0), axis=1
    )
    positions = global_index - start_here
    frequency = 10000.0 ** (-(jnp.arange(HD // 2, dtype=F32) * 2.0 / HD))
    angles = positions.astype(F32)[:, None] * frequency[None, :]
    cosine, sine = jnp.cos(angles), jnp.sin(angles)
    cos_full = jnp.concatenate([cosine, cosine], axis=1)
    sin_full = jnp.concatenate([-sine, sine], axis=1)

    def rotate(values):
        swapped = jnp.concatenate([values[:, HD // 2 :], values[:, : HD // 2]], axis=1)
        return values * cos_full + swapped * sin_full

    widened = tokens.astype(F32)
    normed = (
        widened
        * lax.rsqrt(jnp.mean(widened * widened, axis=1, keepdims=True) + 1e-06)
        * norm_gain.astype(F32)
    ).astype(BF)
    block_width = width // blocks
    block_row = jnp.arange(block_width, dtype=jnp.int32)
    upper_places = block_places(w_rows, 0, 2 * w_rows)
    lower_places = block_places(w_rows, w_rows, 2 * w_rows)
    upper_pick = (block_row[:, None] == upper_places[None, :]).astype(BF)
    lower_pick = (block_row[:, None] == lower_places[None, :]).astype(BF)

    def place(pick):
        return jnp.concatenate(
            [
                jnp.dot(
                    normed[:, k * block_width : (k + 1) * block_width],
                    pick,
                    preferred_element_type=F32,
                ).astype(BF)
                for k in range(blocks)
            ],
            axis=1,
        )

    placed_upper, placed_lower, lower_pick = lax.optimization_barrier(
        (place(upper_pick), place(lower_pick), lower_pick)
    )
    projected = jnp.dot(placed_upper, gathered, preferred_element_type=F32)
    values = jnp.dot(placed_lower, gathered[:, :HD], preferred_element_type=F32)
    pairs = jnp.concatenate([rotate(projected[:, q_cols:]), values], axis=1).astype(BF)

    slots_here = WINDOW // devices
    col_share = kv_cols // n_head
    first_segment = jnp.sum((prompt_ends <= tok_index * shard_rows).astype(jnp.int32))
    slot_index = jnp.arange(WINDOW, dtype=jnp.int32)
    share = lax.dynamic_slice_in_dim(pairs, head_index * col_share, col_share, 1)
    picks = []
    for local_seg in range(2):
        prompt_here = first_segment + local_seg
        matches = prompt_index == prompt_here
        prompt_size = jnp.sum(jnp.where(matches, lengths, 0))
        prompt_start = jnp.sum(jnp.where(matches, starts, 0))
        lowest = prompt_size - WINDOW
        places = lowest + jnp.mod(slot_index - lowest, WINDOW)
        local_rows = prompt_start + places - tok_index * shard_rows
        usable = (prompt_here < prompts) & (places >= 0)
        local_rows = jnp.where(usable, local_rows, -1)
        picks.append(local_rows[:, None] == jnp.arange(shard_rows, dtype=jnp.int32)[None, :])
    pick = jnp.concatenate(picks, axis=1).astype(BF)
    blank = jnp.zeros_like(share)
    shares = jnp.concatenate(
        [jnp.concatenate([share, blank], axis=1), jnp.concatenate([blank, share], axis=1)], axis=0
    )
    outgoing = jnp.dot(pick, shares, preferred_element_type=F32).astype(BF)
    outgoing = outgoing.reshape(devices, slots_here, 2 * col_share)
    incoming = lax.all_to_all(outgoing, TOK, 0, 0, tiled=True)

    chip_reach = -(-WINDOW // (2 * shard_rows))
    behind = [earlier(pairs, 2 * k) for k in range(chip_reach, 0, -1)] + [pairs]
    own_keys = jnp.concatenate(behind, axis=0)
    other_keys = swap(own_keys)
    all_pairs = jnp.concatenate([own_keys, other_keys], axis=0)
    core = lax.axis_index("c")
    own_chip = tok_index // 2
    key_place = jnp.arange(2 * (chip_reach + 1) * shard_rows, dtype=jnp.int32)
    key_block = key_place // shard_rows
    key_chip = own_chip - chip_reach + key_block % (chip_reach + 1)
    key_core = core ^ (key_block // (chip_reach + 1))
    key_index = (2 * key_chip + key_core) * shard_rows + key_place % shard_rows

    queries = jnp.concatenate(
        [rotate(projected[:, s * HD : (s + 1) * HD]) for s in range(heads_here)], axis=0
    ).astype(BF)
    scores = lax.dot_general(
        queries, all_pairs[:, :HD], (((1,), (1,)), ((), ())), preferred_element_type=F32
    ) * (1.0 / math.sqrt(HD))
    allowed = (
        (key_index[None, :] >= start_here[:, None])
        & (key_index[None, :] <= global_index[:, None])
        & (key_index[None, :] > global_index[:, None] - WINDOW)
        & (key_index[None, :] >= 0)
    )
    scores = scores.reshape(heads_here, shard_rows, -1)
    scores = jnp.where(allowed[None], scores, -jnp.inf)
    largest = jnp.max(scores, axis=2, keepdims=True)
    weights = jnp.exp(scores - largest)
    total = jnp.sum(weights, axis=2, keepdims=True)
    probs = weights.astype(BF).reshape(heads_here * shard_rows, -1)
    summed = jnp.dot(probs, all_pairs[:, HD:], preferred_element_type=F32)
    attention = (summed / total.reshape(-1, 1)).astype(BF)
    attention = jnp.concatenate(
        [attention[s * shard_rows : (s + 1) * shard_rows] for s in range(heads_here)], axis=1
    )

    source_rows = jnp.arange(devices, dtype=jnp.int32) * shard_rows
    source_first = jnp.sum((prompt_ends[None, :] <= source_rows[:, None]).astype(jnp.int32), axis=1)
    table_rows = 32
    table_index = jnp.arange(table_rows, dtype=jnp.int32)
    table = jnp.zeros((table_rows, slots_here, col_share), F32)
    for local_seg in range(2):
        chooser = (source_first[None, :] + local_seg == table_index[:, None]).astype(BF)
        table = table + jnp.einsum(
            "ps,sjl->pjl",
            chooser,
            incoming[:, :, local_seg * col_share : (local_seg + 1) * col_share],
            preferred_element_type=F32,
        )
    table = table.astype(BF).reshape(shard_rows, -1)

    partial_out = lax.dot_general(
        attention, gathered[:, HD:], (((1,), (1,)), ((), ())), preferred_element_type=F32
    ).astype(BF)
    block_places_width = partial_out.shape[1] // blocks
    partial_out = jnp.concatenate(
        [
            lax.dot_general(
                partial_out[:, k * block_places_width : (k + 1) * block_places_width],
                lower_pick,
                (((1,), (1,)), ((), ())),
                preferred_element_type=F32,
            ).astype(BF)
            for k in range(blocks)
        ],
        axis=1,
    )
    quarter_cols = width // n_head
    sending = jnp.stack(
        [
            jnp.concatenate([partial_out[:, k * quarter_cols : (k + 1) * quarter_cols], table], axis=1)
            for k in range(n_head)
        ]
    )
    arrived = lax.all_to_all(sending, "head", 0, 0, tiled=True)
    residual = lax.dynamic_slice_in_dim(tokens, head_index * quarter_cols, quarter_cols, 1)
    mixed = (
        residual.astype(F32) + jnp.sum(arrived[:, :, :quarter_cols].astype(F32), axis=0)
    ).astype(BF)

    slot_table = arrived[:, :, quarter_cols:].reshape(n_head, table_rows, slots_here, col_share)
    member_pick = (member_prompt[:, None] == table_index[None, :]).astype(BF)
    cycle_cache = jnp.einsum("mp,hpjl->mjhl", member_pick, slot_table, preferred_element_type=F32)
    cycle_cache = cycle_cache.astype(BF).reshape(member_prompt.shape[0], slots_here, kv_cols)
    return (mixed, cycle_cache)


def solution(mesh):
    cut = Mesh(mesh.devices.reshape(4, 2, 4, 2, 2, 4), TOK + ("head",))
    return jax.shard_map(
        layer,
        mesh=cut,
        in_specs=(
            P(TOK, None),
            P(),
            P(TOK, "head"),
            P(TOK, None),
            P("head", TOK),
            P(TOK),
            P(),
            P("head"),
        ),
        out_specs=(P(TOK, "head"), P("head", TOK, None)),
        check_vma=False,
    )
```

```python
import math

import jax
import jax.numpy as jnp
from jax import lax
from jax.sharding import Mesh, PartitionSpec as P


HD = 128
WINDOW = 1024
TOK = ("zh", "zl", "yh", "yl", "c")
BF = jnp.bfloat16
F32 = jnp.float32


def swap(x):
    return lax.ppermute(x, "c", [(0, 1), (1, 0)])


def earlier(x, distance):
    size = lax.axis_size(TOK)
    return lax.ppermute(x, TOK, [(i, i + distance) for i in range(size - distance)])


def gather_rows(chunk):
    line = ("zh", "zl", "c")
    members = lax.axis_size(line)
    n_zh = lax.axis_size("zh")
    n_y = lax.axis_size(("yh", "yl"))
    half = members // 2
    core = lax.axis_index("c")
    own = lax.all_to_all(
        jnp.broadcast_to(chunk[None], (members,) + chunk.shape), line, 0, 0, tiled=True
    )
    route = [(2 * y, 2 * ((y + 1) % n_y)) for y in range(n_y)]
    route += [(2 * y + 1, 2 * ((y - 1) % n_y) + 1) for y in range(n_y)]

    def onward(block):
        return lax.ppermute(block, ("yh", "yl", "c"), route)

    moving = own
    walked, swapped = [], []
    for _ in range(n_y // 2 - 1):
        moving = onward(moving)
        walked.append(moving)
        swapped.append(swap(moving))
    last = onward(lax.dynamic_slice_in_dim(moving, core * half, half, 0))
    last_swapped = swap(last)
    far = jnp.concatenate(
        [
            jnp.where(core == 0, last, last_swapped),
            jnp.where(core == 0, last_swapped, last),
        ],
        axis=0,
    )
    shape = (n_zh, members // n_zh) + chunk.shape
    pieces = [piece.reshape(shape) for piece in [own] + walked + swapped + [far]]
    return jnp.stack(pieces, axis=1)


def block_places(rows, offset, stacked):
    core = lax.axis_index("c")
    here = lax.axis_index(("yh", "yl"))
    n_zl, n_y = lax.axis_size("zl"), lax.axis_size(("yh", "yl"))
    steps = n_y // 2 - 1
    place = jnp.arange(n_y * n_zl * 2 * stacked, dtype=jnp.int32)
    row = place % stacked - offset
    of_core = (place // stacked) % 2
    zl = (place // (stacked * 2)) % n_zl
    piece = place // (stacked * 2 * n_zl)
    distance = jnp.where(piece <= steps, -piece, piece - steps)
    y = (here + jnp.where(core == 0, distance, -distance)) % n_y
    device = (zl * n_y + y) * 2 + of_core
    return jnp.where((row >= 0) & (row < rows), device * rows + row, -1)


def layer(tokens, norm_gain, w_query, w_keyval, w_out, segment_ids, lengths, member_prompt):
    shard_rows, width = tokens.shape
    q_cols = w_query.shape[1]
    kv_cols = w_keyval.shape[1]
    heads_here = q_cols // HD
    devices = lax.axis_size(TOK)
    n_head = lax.axis_size("head")
    tok_index = lax.axis_index(TOK)
    head_index = lax.axis_index("head")
    prompts = lengths.shape[0]
    w_rows = w_query.shape[0]

    upper = jnp.concatenate([w_query, w_keyval[:, :HD]], axis=1)
    lower = jnp.concatenate([w_keyval[:, HD:], w_out.T], axis=1)
    chunk = jnp.concatenate([upper, lower], axis=0)
    blocks = lax.axis_size("zh")
    gathered = gather_rows(chunk).reshape(-1, chunk.shape[1])

    prompt_ends = jnp.cumsum(lengths)
    starts = prompt_ends - lengths
    global_index = tok_index * shard_rows + jnp.arange(shard_rows, dtype=jnp.int32)
    prompt_index = jnp.arange(prompts, dtype=jnp.int32)
    start_here = jnp.sum(
        jnp.where(segment_ids[:, None] == prompt_index[None, :], starts[None, :], 0), axis=1
    )
    positions = global_index - start_here
    frequency = 10000.0 ** (-(jnp.arange(HD // 2, dtype=F32) * 2.0 / HD))
    angles = positions.astype(F32)[:, None] * frequency[None, :]
    cosine, sine = jnp.cos(angles), jnp.sin(angles)
    cos_full = jnp.concatenate([cosine, cosine], axis=1)
    sin_full = jnp.concatenate([-sine, sine], axis=1)

    def rotate(values):
        swapped = jnp.concatenate([values[:, HD // 2 :], values[:, : HD // 2]], axis=1)
        return values * cos_full + swapped * sin_full

    widened = tokens.astype(F32)
    normed = (
        widened
        * lax.rsqrt(jnp.mean(widened * widened, axis=1, keepdims=True) + 1e-06)
        * norm_gain.astype(F32)
    ).astype(BF)
    block_width = width // blocks
    block_row = jnp.arange(block_width, dtype=jnp.int32)
    upper_places = block_places(w_rows, 0, 2 * w_rows)
    lower_places = block_places(w_rows, w_rows, 2 * w_rows)
    upper_pick = (block_row[:, None] == upper_places[None, :]).astype(BF)
    lower_pick = (block_row[:, None] == lower_places[None, :]).astype(BF)

    def place(pick):
        return jnp.concatenate(
            [
                jnp.dot(
                    normed[:, k * block_width : (k + 1) * block_width],
                    pick,
                    preferred_element_type=F32,
                ).astype(BF)
                for k in range(blocks)
            ],
            axis=1,
        )

    placed_upper, placed_lower, lower_pick = lax.optimization_barrier(
        (place(upper_pick), place(lower_pick), lower_pick)
    )
    projected = jnp.dot(placed_upper, gathered, preferred_element_type=F32)
    values = jnp.dot(placed_lower, gathered[:, :HD], preferred_element_type=F32)
    pairs = jnp.concatenate([rotate(projected[:, q_cols:]), values], axis=1).astype(BF)

    slots_here = WINDOW // devices
    col_share = kv_cols // n_head
    first_segment = jnp.sum((prompt_ends <= tok_index * shard_rows).astype(jnp.int32))
    slot_index = jnp.arange(WINDOW, dtype=jnp.int32)
    share = lax.dynamic_slice_in_dim(pairs, head_index * col_share, col_share, 1)
    picks = []
    for local_seg in range(2):
        prompt_here = first_segment + local_seg
        matches = prompt_index == prompt_here
        prompt_size = jnp.sum(jnp.where(matches, lengths, 0))
        prompt_start = jnp.sum(jnp.where(matches, starts, 0))
        lowest = prompt_size - WINDOW
        places = lowest + jnp.mod(slot_index - lowest, WINDOW)
        local_rows = prompt_start + places - tok_index * shard_rows
        usable = (prompt_here < prompts) & (places >= 0)
        local_rows = jnp.where(usable, local_rows, -1)
        picks.append(local_rows[:, None] == jnp.arange(shard_rows, dtype=jnp.int32)[None, :])
    pick = jnp.concatenate(picks, axis=1).astype(BF)
    blank = jnp.zeros_like(share)
    shares = jnp.concatenate(
        [jnp.concatenate([share, blank], axis=1), jnp.concatenate([blank, share], axis=1)], axis=0
    )
    outgoing = jnp.dot(pick, shares, preferred_element_type=F32).astype(BF)
    outgoing = outgoing.reshape(devices, slots_here, 2 * col_share)
    incoming = lax.all_to_all(outgoing, TOK, 0, 0, tiled=True)

    chip_reach = -(-WINDOW // (2 * shard_rows))
    behind = [earlier(pairs, 2 * k) for k in range(chip_reach, 0, -1)] + [pairs]
    own_keys = jnp.concatenate(behind, axis=0)
    other_keys = swap(own_keys)
    all_pairs = jnp.concatenate([own_keys, other_keys], axis=0)
    core = lax.axis_index("c")
    own_chip = tok_index // 2
    key_place = jnp.arange(2 * (chip_reach + 1) * shard_rows, dtype=jnp.int32)
    key_block = key_place // shard_rows
    key_chip = own_chip - chip_reach + key_block % (chip_reach + 1)
    key_core = core ^ (key_block // (chip_reach + 1))
    key_index = (2 * key_chip + key_core) * shard_rows + key_place % shard_rows

    queries = jnp.concatenate(
        [rotate(projected[:, s * HD : (s + 1) * HD]) for s in range(heads_here)], axis=0
    ).astype(BF)
    scores = lax.dot_general(
        queries, all_pairs[:, :HD], (((1,), (1,)), ((), ())), preferred_element_type=F32
    ) * (1.0 / math.sqrt(HD))
    allowed = (
        (key_index[None, :] >= start_here[:, None])
        & (key_index[None, :] <= global_index[:, None])
        & (key_index[None, :] > global_index[:, None] - WINDOW)
        & (key_index[None, :] >= 0)
    )
    scores = scores.reshape(heads_here, shard_rows, -1)
    scores = jnp.where(allowed[None], scores, -jnp.inf)
    largest = jnp.max(scores, axis=2, keepdims=True)
    weights = jnp.exp(scores - largest)
    total = jnp.sum(weights, axis=2, keepdims=True)
    probs = weights.astype(BF).reshape(heads_here * shard_rows, -1)
    summed = jnp.dot(probs, all_pairs[:, HD:], preferred_element_type=F32)
    attention = (summed / total.reshape(-1, 1)).astype(BF)
    attention = jnp.concatenate(
        [attention[s * shard_rows : (s + 1) * shard_rows] for s in range(heads_here)], axis=1
    )

    source_rows = jnp.arange(devices, dtype=jnp.int32) * shard_rows
    source_first = jnp.sum((prompt_ends[None, :] <= source_rows[:, None]).astype(jnp.int32), axis=1)
    table_rows = 32
    table_index = jnp.arange(table_rows, dtype=jnp.int32)
    table = jnp.zeros((table_rows, slots_here, col_share), F32)
    for local_seg in range(2):
        chooser = (source_first[None, :] + local_seg == table_index[:, None]).astype(BF)
        table = table + jnp.einsum(
            "ps,sjl->pjl",
            chooser,
            incoming[:, :, local_seg * col_share : (local_seg + 1) * col_share],
            preferred_element_type=F32,
        )
    table = table.astype(BF).reshape(shard_rows, -1)

    partial_out = lax.dot_general(
        attention, gathered[:, HD:], (((1,), (1,)), ((), ())), preferred_element_type=F32
    ).astype(BF)
    block_places_width = partial_out.shape[1] // blocks
    partial_out = jnp.concatenate(
        [
            lax.dot_general(
                partial_out[:, k * block_places_width : (k + 1) * block_places_width],
                lower_pick,
                (((1,), (1,)), ((), ())),
                preferred_element_type=F32,
            ).astype(BF)
            for k in range(blocks)
        ],
        axis=1,
    )
    quarter_cols = width // n_head
    sending = jnp.stack(
        [
            jnp.concatenate([partial_out[:, k * quarter_cols : (k + 1) * quarter_cols], table], axis=1)
            for k in range(n_head)
        ]
    )
    arrived = lax.all_to_all(sending, "head", 0, 0, tiled=True)
    residual = lax.dynamic_slice_in_dim(tokens, head_index * quarter_cols, quarter_cols, 1)
    mixed = (
        residual.astype(F32) + jnp.sum(arrived[:, :, :quarter_cols].astype(F32), axis=0)
    ).astype(BF)

    slot_table = arrived[:, :, quarter_cols:].reshape(n_head, table_rows, slots_here, col_share)
    member_pick = (member_prompt[:, None] == table_index[None, :]).astype(BF)
    cycle_cache = jnp.einsum("mp,hpjl->mjhl", member_pick, slot_table, preferred_element_type=F32)
    cycle_cache = cycle_cache.astype(BF).reshape(member_prompt.shape[0], slots_here, kv_cols)
    return (mixed, cycle_cache)


def solution(mesh):
    cut = Mesh(mesh.devices.reshape(4, 2, 4, 2, 2, 4), TOK + ("head",))
    return jax.shard_map(
        layer,
        mesh=cut,
        in_specs=(
            P(TOK, None),
            P(),
            P(TOK, "head"),
            P(TOK, None),
            P("head", TOK),
            P(TOK),
            P(),
            P("head"),
        ),
        out_specs=(P(TOK, "head"), P("head", TOK, None)),
        check_vma=False,
    )
```

```python
import math

import jax
import jax.numpy as jnp
from jax import lax
from jax.sharding import Mesh, PartitionSpec as P


HD = 128
WINDOW = 1024
TOK = ("zh", "zl", "yh", "yl", "c")
BF = jnp.bfloat16
F32 = jnp.float32


def ring(x, axes, step):
    size = lax.axis_size(axes)
    return lax.ppermute(x, axes, [(i, (i + step) % size) for i in range(size)])


def swap(x):
    return lax.ppermute(x, "c", [(0, 1), (1, 0)])


def earlier(x, distance):
    size = lax.axis_size(TOK)
    return lax.ppermute(x, TOK, [(i, i + distance) for i in range(size - distance)])


def gather_rows(chunk):
    line = ("zh", "zl", "yh")
    members = lax.axis_size(line)
    n_zh = lax.axis_size("zh")
    half = members // 2
    own = lax.all_to_all(
        jnp.broadcast_to(chunk[None], (members,) + chunk.shape), line, 0, 0, tiled=True
    )
    below = ring(own[:half], ("yh", "yl"), 1)
    own_swapped = swap(own)
    above = ring(own[half:], ("yh", "yl"), -1)
    below_swapped = swap(below)
    above_swapped = swap(above)
    shape = (n_zh // 2, members // n_zh) + chunk.shape
    first = [own[:half], below, own_swapped[:half], below_swapped]
    second = [own[half:], above, own_swapped[half:], above_swapped]
    return jnp.concatenate(
        [jnp.stack([part.reshape(shape) for part in parts], axis=1) for parts in (first, second)],
        axis=0,
    )


def block_places(rows, offset, stacked):
    yl, core = lax.axis_index("yl"), lax.axis_index("c")
    n_zl, n_yh = lax.axis_size("zl"), lax.axis_size("yh")
    place = jnp.arange(4 * n_zl * n_yh * stacked, dtype=jnp.int32)
    row = place % stacked - offset
    yh = (place // stacked) % n_yh
    zl = (place // (stacked * n_yh)) % n_zl
    piece = place // (stacked * n_yh * n_zl)
    y = 2 * yh + (yl ^ (piece % 2))
    device = (zl * (2 * n_yh) + y) * 2 + (core ^ (piece // 2))
    return jnp.where((row >= 0) & (row < rows), device * rows + row, -1)


def layer(tokens, norm_gain, w_query, w_keyval, w_out, segment_ids, lengths, member_prompt):
    shard_rows, width = tokens.shape
    q_cols = w_query.shape[1]
    kv_cols = w_keyval.shape[1]
    heads_here = q_cols // HD
    devices = lax.axis_size(TOK)
    n_head = lax.axis_size("head")
    tok_index = lax.axis_index(TOK)
    head_index = lax.axis_index("head")
    prompts = lengths.shape[0]
    w_rows = w_query.shape[0]

    upper = jnp.concatenate([w_query, w_keyval[:, :HD]], axis=1)
    lower = jnp.concatenate([w_keyval[:, HD:], w_out.T], axis=1)
    chunk = jnp.concatenate([upper, lower], axis=0)
    blocks = lax.axis_size("zh")
    gathered = gather_rows(chunk).reshape(-1, chunk.shape[1])

    prompt_ends = jnp.cumsum(lengths)
    starts = prompt_ends - lengths
    global_index = tok_index * shard_rows + jnp.arange(shard_rows, dtype=jnp.int32)
    prompt_index = jnp.arange(prompts, dtype=jnp.int32)
    start_here = jnp.sum(
        jnp.where(segment_ids[:, None] == prompt_index[None, :], starts[None, :], 0), axis=1
    )
    positions = global_index - start_here
    frequency = 10000.0 ** (-(jnp.arange(HD // 2, dtype=F32) * 2.0 / HD))
    angles = positions.astype(F32)[:, None] * frequency[None, :]
    cosine, sine = jnp.cos(angles), jnp.sin(angles)
    cos_full = jnp.concatenate([cosine, cosine], axis=1)
    sin_full = jnp.concatenate([-sine, sine], axis=1)

    def rotate(values):
        swapped = jnp.concatenate([values[:, HD // 2 :], values[:, : HD // 2]], axis=1)
        return values * cos_full + swapped * sin_full

    widened = tokens.astype(F32)
    normed = (
        widened
        * lax.rsqrt(jnp.mean(widened * widened, axis=1, keepdims=True) + 1e-06)
        * norm_gain.astype(F32)
    ).astype(BF)
    block_width = width // blocks
    block_row = jnp.arange(block_width, dtype=jnp.int32)
    upper_places = block_places(w_rows, 0, 2 * w_rows)
    lower_places = block_places(w_rows, w_rows, 2 * w_rows)
    upper_pick = (block_row[:, None] == upper_places[None, :]).astype(BF)
    lower_pick = (block_row[:, None] == lower_places[None, :]).astype(BF)

    def place(pick):
        return jnp.concatenate(
            [
                jnp.dot(
                    normed[:, k * block_width : (k + 1) * block_width],
                    pick,
                    preferred_element_type=F32,
                ).astype(BF)
                for k in range(blocks)
            ],
            axis=1,
        )

    placed_upper, placed_lower, lower_pick = lax.optimization_barrier(
        (place(upper_pick), place(lower_pick), lower_pick)
    )
    projected = jnp.dot(placed_upper, gathered, preferred_element_type=F32)
    values = jnp.dot(placed_lower, gathered[:, :HD], preferred_element_type=F32)
    pairs = jnp.concatenate([rotate(projected[:, q_cols:]), values], axis=1).astype(BF)

    slots_here = WINDOW // devices
    col_share = kv_cols // n_head
    first_segment = jnp.sum((prompt_ends <= tok_index * shard_rows).astype(jnp.int32))
    slot_index = jnp.arange(WINDOW, dtype=jnp.int32)
    share = lax.dynamic_slice_in_dim(pairs, head_index * col_share, col_share, 1)
    picks = []
    for local_seg in range(2):
        prompt_here = first_segment + local_seg
        matches = prompt_index == prompt_here
        prompt_size = jnp.sum(jnp.where(matches, lengths, 0))
        prompt_start = jnp.sum(jnp.where(matches, starts, 0))
        lowest = prompt_size - WINDOW
        places = lowest + jnp.mod(slot_index - lowest, WINDOW)
        local_rows = prompt_start + places - tok_index * shard_rows
        usable = (prompt_here < prompts) & (places >= 0)
        local_rows = jnp.where(usable, local_rows, -1)
        picks.append(local_rows[:, None] == jnp.arange(shard_rows, dtype=jnp.int32)[None, :])
    pick = jnp.concatenate(picks, axis=1).astype(BF)
    blank = jnp.zeros_like(share)
    shares = jnp.concatenate(
        [jnp.concatenate([share, blank], axis=1), jnp.concatenate([blank, share], axis=1)], axis=0
    )
    outgoing = jnp.dot(pick, shares, preferred_element_type=F32).astype(BF)
    outgoing = outgoing.reshape(devices, slots_here, 2 * col_share)
    incoming = lax.all_to_all(outgoing, TOK, 0, 0, tiled=True)

    chip_reach = -(-WINDOW // (2 * shard_rows))
    behind = [earlier(pairs, 2 * k) for k in range(chip_reach, 0, -1)] + [pairs]
    own_keys = jnp.concatenate(behind, axis=0)
    other_keys = swap(own_keys)
    all_pairs = jnp.concatenate([own_keys, other_keys], axis=0)
    core = lax.axis_index("c")
    own_chip = tok_index // 2
    key_place = jnp.arange(2 * (chip_reach + 1) * shard_rows, dtype=jnp.int32)
    key_block = key_place // shard_rows
    key_chip = own_chip - chip_reach + key_block % (chip_reach + 1)
    key_core = core ^ (key_block // (chip_reach + 1))
    key_index = (2 * key_chip + key_core) * shard_rows + key_place % shard_rows

    queries = jnp.concatenate(
        [rotate(projected[:, s * HD : (s + 1) * HD]) for s in range(heads_here)], axis=0
    ).astype(BF)
    scores = lax.dot_general(
        queries, all_pairs[:, :HD], (((1,), (1,)), ((), ())), preferred_element_type=F32
    ) * (1.0 / math.sqrt(HD))
    allowed = (
        (key_index[None, :] >= start_here[:, None])
        & (key_index[None, :] <= global_index[:, None])
        & (key_index[None, :] > global_index[:, None] - WINDOW)
        & (key_index[None, :] >= 0)
    )
    scores = scores.reshape(heads_here, shard_rows, -1)
    scores = jnp.where(allowed[None], scores, -jnp.inf)
    largest = jnp.max(scores, axis=2, keepdims=True)
    weights = jnp.exp(scores - largest)
    total = jnp.sum(weights, axis=2, keepdims=True)
    probs = weights.astype(BF).reshape(heads_here * shard_rows, -1)
    summed = jnp.dot(probs, all_pairs[:, HD:], preferred_element_type=F32)
    attention = (summed / total.reshape(-1, 1)).astype(BF)
    attention = jnp.concatenate(
        [attention[s * shard_rows : (s + 1) * shard_rows] for s in range(heads_here)], axis=1
    )

    source_rows = jnp.arange(devices, dtype=jnp.int32) * shard_rows
    source_first = jnp.sum((prompt_ends[None, :] <= source_rows[:, None]).astype(jnp.int32), axis=1)
    table_rows = 32
    table_index = jnp.arange(table_rows, dtype=jnp.int32)
    table = jnp.zeros((table_rows, slots_here, col_share), F32)
    for local_seg in range(2):
        chooser = (source_first[None, :] + local_seg == table_index[:, None]).astype(BF)
        table = table + jnp.einsum(
            "ps,sjl->pjl",
            chooser,
            incoming[:, :, local_seg * col_share : (local_seg + 1) * col_share],
            preferred_element_type=F32,
        )
    table = table.astype(BF).reshape(shard_rows, -1)

    partial_out = lax.dot_general(
        attention, gathered[:, HD:], (((1,), (1,)), ((), ())), preferred_element_type=F32
    ).astype(BF)
    block_places_width = partial_out.shape[1] // blocks
    partial_out = jnp.concatenate(
        [
            lax.dot_general(
                partial_out[:, k * block_places_width : (k + 1) * block_places_width],
                lower_pick,
                (((1,), (1,)), ((), ())),
                preferred_element_type=F32,
            ).astype(BF)
            for k in range(blocks)
        ],
        axis=1,
    )
    quarter_cols = width // n_head
    sending = jnp.stack(
        [
            jnp.concatenate([partial_out[:, k * quarter_cols : (k + 1) * quarter_cols], table], axis=1)
            for k in range(n_head)
        ]
    )
    arrived = lax.all_to_all(sending, "head", 0, 0, tiled=True)
    residual = lax.dynamic_slice_in_dim(tokens, head_index * quarter_cols, quarter_cols, 1)
    mixed = (
        residual.astype(F32) + jnp.sum(arrived[:, :, :quarter_cols].astype(F32), axis=0)
    ).astype(BF)

    slot_table = arrived[:, :, quarter_cols:].reshape(n_head, table_rows, slots_here, col_share)
    member_pick = (member_prompt[:, None] == table_index[None, :]).astype(BF)
    cycle_cache = jnp.einsum("mp,hpjl->mjhl", member_pick, slot_table, preferred_element_type=F32)
    cycle_cache = cycle_cache.astype(BF).reshape(member_prompt.shape[0], slots_here, kv_cols)
    return (mixed, cycle_cache)


def solution(mesh):
    cut = Mesh(mesh.devices.reshape(4, 2, 4, 2, 2, 4), TOK + ("head",))
    return jax.shard_map(
        layer,
        mesh=cut,
        in_specs=(
            P(TOK, None),
            P(),
            P(TOK, "head"),
            P(TOK, None),
            P("head", TOK),
            P(TOK),
            P(),
            P("head"),
        ),
        out_specs=(P(TOK, "head"), P("head", TOK, None)),
        check_vma=False,
    )
```
